128 devices in a mesh: req: 32 (over x, y, core), mlp: 4 (over z).
Axes of the slice: x: 4, y: 4, z: 4, core: 2. Of those that a mesh axis runs over, the one named last changes fastest.
Arguments:
- tokens: bfloat16 [1024, 2048], P('req'), may hold values from -6 to 6
- prefix_len: int32 [32], replicated, may hold values from 1 to 4096, 65536 in all
- tail_len: int32 [32, 16], replicated, may hold values from 1 to 64, 512 in all within a row
- tail_src: int32 [512], replicated, may hold values from 0 to 31, as said below
- prefix_kv: bfloat16 [32, 2, 4096, 2048], P('req', None, None, 'mlp'), may hold values from -256 to 256, as said below
- tail_kv: bfloat16 [512, 2, 64, 2048], P('req', None, None, 'mlp'), may hold values from -256 to 256, as said below
- w_qkv: bfloat16 [2048, 3, 2048], P(None, None, 'mlp'), may hold values from -0.125 to 0.125
- w_out: bfloat16 [2048, 2048], P('mlp'), may hold values from -0.125 to 0.125
- w_gate: bfloat16 [8192, 2048], P(('req', 'mlp')), may hold values from -0.125 to 0.125
- w_up: bfloat16 [8192, 2048], P(('req', 'mlp')), may hold values from -0.125 to 0.125
- w_down: bfloat16 [8192, 2048], P(('req', 'mlp')), may hold values from -0.0625 to 0.0625
- w_score: float32 [2048], replicated, may hold values from -0.125 to 0.125
Outputs:
- layer_out: bfloat16 [1024, 2048], P(('req', 'mlp'))
- score: float32 [1024], P(('req', 'mlp'))
The draws below stay inside these ranges and needn't reach their ends.
Inputs may be any that keep to these rules, and one draw needn't show every extreme that they name: tail_src[c] is the req index whose shard of tail_kv holds the tail of continuation c; each device holds 16 tails, in increasing order of continuation. The 16 continuations of a prompt come in groups of 1 from 16 different devices, so from one device to the device of one prompt goes exactly one tail or none. `prefix_kv`: keys are already rotated. `tail_kv`: keys are already rotated.
All inputs are finite; a program needn't handle non-finite values.
Results may differ from the reference program's by a relative error of at most 0.027.
Values may be sent and summed in bfloat16 or wider, within the bound.
A program may use at most 128 MiB of HBM per device.

```python
import math
from functools import reduce
import jax
import jax.numpy as jnp
import numpy as np
from jax import lax

D = 2048
HEADS = 16
HEAD_DIM = 128
FF = 8192
CONT = 16
NEW = 2
PREFIX = 4096
TAILMAX = 64
CAP = 1
PROMPTS = 32
CONTS = 512
TOKENS = 1024


def draw_cache(key, shape):
    spin_wavelength = jnp.clip(jax.random.normal(jax.random.fold_in(key, 1), shape, jnp.float32), -4.0, 4.0)
    return spin_wavelength


def draw_prefix_kv(key, part):
    return draw_cache(key, (PROMPTS, 2, PREFIX, HEADS * HEAD_DIM)).astype(jnp.bfloat16)


def draw_tail_kv(key, part):
    return draw_cache(key, (CONTS, 2, TAILMAX, HEADS * HEAD_DIM)).astype(jnp.bfloat16)


def shuffle_one(sub_key):
    return jax.random.permutation(sub_key, CONT)


def draw_tail_src(key, part):
    offsets = jax.random.permutation(jax.random.fold_in(key, 11), PROMPTS)[:CONT // CAP]
    prompt_keys = jax.random.split(jax.random.fold_in(key, 12), PROMPTS)
    orders = jax.vmap(shuffle_one)(prompt_keys)
    prompt_ids = jnp.arange(PROMPTS, dtype=jnp.int32)[:, None]
    source_rows = (prompt_ids + offsets[orders // CAP]) % PROMPTS
    return source_rows.reshape(-1).astype(jnp.int32)


def block_scale(stream_key, extent, cuts, smallest, top_value):
    def one(dim, blocks):
        steps = jax.random.uniform(jax.random.fold_in(jax.random.fold_in(stream_key, 6), dim), (blocks,), jnp.float32, smallest / len(cuts), top_value / len(cuts))
        return jnp.repeat(jnp.exp(steps), extent[dim] // blocks).reshape((-1,) + (1,) * (len(extent) - dim - 1))

    factor_of = one(*cuts[0])
    for cut in cuts[1:]:
        factor_of = factor_of * one(*cut)
    return factor_of


def profile(amount, total, limit, slope):
    loads = [(1 << 20) // math.isqrt(standing ** slope) + 1 for standing in range(2, amount + 1)]
    spare, counts = total - limit - (amount - 1), [1] * (amount - 1)
    while spare > 0:
        candidates = [i for i in range(amount - 1) if counts[i] < limit]
        mass, budget = sum([loads[i] for i in candidates]), spare
        for i in candidates:
            extra = min(limit - counts[i], max(1, budget * loads[i] // mass), spare)
            counts[i] = counts[i] + extra
            spare = spare - extra
    return np.array([limit] + counts)


def uneven(stream_key, count, total, limit, slope):
    if count == 2:
        one = jax.random.randint(stream_key, (), max(1, total - limit), min(limit, total - 1) + 1)
        return jnp.stack([one, total - one])
    tallies = jnp.asarray(profile(count, total, limit, slope), jnp.int32)
    couples = (count - 1) // 2
    donor, taker = tallies[1:1 + 2 * couples:2], tallies[2:2 + 2 * couples:2]
    room = jnp.minimum(donor - 1, limit - taker)
    passed = jax.random.randint(jax.random.fold_in(stream_key, 1), (couples,), 0, 1 << 20) % (room + 1)
    tallies = tallies.at[1:1 + 2 * couples:2].set(donor - passed).at[2:2 + 2 * couples:2].set(taker + passed)
    return tallies[jax.random.permutation(jax.random.fold_in(stream_key, 2), count)]


def gaussian(key, dims, scale, limit, shards=(), kind=jnp.bfloat16):
    array = jax.random.normal(key, dims, jnp.float32) * scale
    if len(shards) > 0:
        array = block_scale(key, dims, shards, -0.22, 0.18) * array
    return jnp.clip(array, min=-limit, max=limit).astype(kind)


def setup_inputs(seed: int = 0) -> dict:
    splits = jax.random.split(jax.random.key(seed), 13)
    tokens = gaussian(splits[0], (TOKENS, D), 1.0, 6.0, ((0, 32),))
    prefix_len = uneven(splits[1], PROMPTS, PROMPTS * PREFIX // 2, PREFIX, 2).astype(jnp.int32)
    tail_len = jax.vmap(lambda own: uneven(own, CONT, CONT * TAILMAX // 2, TAILMAX, 2))(jax.random.split(splits[2], PROMPTS)).reshape((PROMPTS, CONT)).astype(jnp.int32)
    tail_src = draw_tail_src(jax.random.fold_in(splits[12], 71), 0)
    prefix_kv = draw_prefix_kv(jax.random.fold_in(splits[12], 71), 0)
    tail_kv = draw_tail_kv(jax.random.fold_in(splits[12], 71), 0)
    w_qkv = gaussian(splits[6], (D, 3, HEADS * HEAD_DIM), D ** -0.5, 0.125, ((2, 4),))
    w_out = gaussian(splits[7], (HEADS * HEAD_DIM, D), (HEADS * HEAD_DIM) ** -0.5, 0.125, ((0, 4),))
    w_gate = gaussian(splits[8], (FF, D), D ** -0.5, 0.125, ((0, 128),))
    w_up = gaussian(splits[9], (FF, D), D ** -0.5, 0.125, ((0, 128),))
    w_down = gaussian(splits[10], (FF, D), FF ** -0.5, 0.0625, ((0, 128),))
    w_score = gaussian(splits[11], (D,), D ** -0.5, 0.125, (), jnp.float32)
    return dict(tokens=tokens, prefix_len=prefix_len, tail_len=tail_len, tail_src=tail_src, prefix_kv=prefix_kv, tail_kv=tail_kv, w_qkv=w_qkv, w_out=w_out, w_gate=w_gate, w_up=w_up, w_down=w_down, w_score=w_score)


def layer_norm(values):
    centre = values - lax.optimization_barrier(jnp.mean(values, axis=-1, keepdims=True))
    spread = lax.optimization_barrier(jnp.mean(centre * centre, axis=-1, keepdims=True))
    return centre * lax.rsqrt(spread + 1e-05)

def rotate(vectors, positions):
    half_dim = vectors.shape[-1] // 2
    exponent = jnp.arange(half_dim, dtype=jnp.float32) * (2.0 / vectors.shape[-1])
    frequency = jnp.power(10000.0, -exponent)
    phase_radians = positions.astype(jnp.float32)[:, None] * frequency[None, :]
    cosine = jnp.cos(phase_radians)[:, None, :]
    sine_part = jnp.sin(phase_radians)[:, None, :]
    leading = vectors[..., :half_dim]
    trailing = vectors[..., half_dim:]
    return jnp.concatenate([leading * cosine - trailing * sine_part, trailing * cosine + leading * sine_part], axis=-1)

def attend(queries, key_rows, values, key_mask):
    scaling = queries.shape[-1] ** (-0.5)
    scores = jnp.einsum('cjhe,ckhe->cjhk', queries.astype(jnp.float32), key_rows.astype(jnp.float32)) * scaling
    scores = jnp.where(key_mask, scores, -1e+30)
    row_max = lax.optimization_barrier(jnp.max(scores, axis=-1))
    weights = jnp.where(key_mask, jnp.exp(scores - row_max[..., None]), 0.0)
    row_sum = lax.optimization_barrier(jnp.sum(weights, axis=-1))
    rounded = weights.astype(jnp.bfloat16).astype(jnp.float32)
    output = jnp.einsum('cjhk,ckhe->cjhe', rounded, values.astype(jnp.float32))
    return (row_max, row_sum, output)

def combine(pieces):
    overall = reduce(jnp.maximum, [piece[0] for piece in pieces])
    numerator = jnp.zeros_like(pieces[0][2])
    denominator = jnp.zeros_like(pieces[0][1])
    for piece in pieces:
        scale_factor = jnp.exp(piece[0] - overall)
        numerator = numerator + scale_factor[..., None] * piece[2]
        denominator = denominator + scale_factor * piece[1]
    return numerator / denominator[..., None]

def swiglu(normed, gate_rows, up_rows, down_rows):
    contract = (((1,), (1,)), ((), ()))
    gate_out = lax.dot_general(normed, gate_rows, contract, preferred_element_type=jnp.float32)
    up_out = lax.dot_general(normed, up_rows, contract, preferred_element_type=jnp.float32)
    hidden = (jax.nn.silu(gate_out) * up_out).astype(jnp.bfloat16)
    return jnp.dot(hidden, down_rows, preferred_element_type=jnp.float32)

def reference(tokens, prefix_len, tail_len, tail_src, prefix_kv, tail_kv, w_qkv, w_out, w_gate, w_up, w_down, w_score):
    indices = jnp.arange(CONTS, dtype=jnp.int32)
    earlier = (tail_src[None, :] == tail_src[:, None]) & (indices[None, :] < indices[:, None])
    slot_lookup = tail_src * CONT + lax.optimization_barrier(jnp.sum(earlier.astype(jnp.int32), axis=1))
    head_width = HEADS * HEAD_DIM
    qkv_flat = w_qkv.reshape(D, 3 * head_width)
    per_prompt = CONT * NEW
    grouped = (CONT, NEW, HEADS, HEAD_DIM)

    def one_prompt(prompt):
        prompt_rows = lax.dynamic_slice_in_dim(tokens, prompt * per_prompt, per_prompt, 0)
        normed = layer_norm(prompt_rows.astype(jnp.float32)).astype(jnp.bfloat16)
        projected = jnp.dot(normed, qkv_flat, preferred_element_type=jnp.float32).reshape(per_prompt, 3, HEADS, HEAD_DIM)
        prefix_now = lax.dynamic_index_in_dim(prefix_len, prompt, 0, keepdims=False)
        tail_lens = lax.dynamic_index_in_dim(tail_len, prompt, 0, keepdims=False)
        offsets = jnp.arange(NEW, dtype=jnp.int32)
        positions = (prefix_now + tail_lens[:, None] + offsets[None, :]).reshape(-1)
        queries = rotate(projected[:, 0], positions).astype(jnp.bfloat16)
        new_keys = rotate(projected[:, 1], positions).astype(jnp.bfloat16)
        new_values = projected[:, 2].astype(jnp.bfloat16)
        prefix_cache = lax.dynamic_index_in_dim(prefix_kv, prompt, 0, keepdims=False)
        prefix_keys = prefix_cache[0].reshape(1, PREFIX, HEADS, HEAD_DIM)
        prefix_values = prefix_cache[1].reshape(1, PREFIX, HEADS, HEAD_DIM)
        prefix_mask = (jnp.arange(PREFIX, dtype=jnp.int32) < prefix_now)[None, None, None, :]
        prefix_part = attend(queries.reshape(1, per_prompt, HEADS, HEAD_DIM), prefix_keys, prefix_values, prefix_mask)
        prefix_part = tuple((member.reshape((CONT, NEW) + member.shape[2:]) for member in prefix_part))
        slots = lax.dynamic_slice_in_dim(slot_lookup, prompt * CONT, CONT, 0)
        tail_cache = tail_kv[slots]
        tail_keys = tail_cache[:, 0].reshape(CONT, TAILMAX, HEADS, HEAD_DIM)
        tail_values = tail_cache[:, 1].reshape(CONT, TAILMAX, HEADS, HEAD_DIM)
        tail_mask = (jnp.arange(TAILMAX, dtype=jnp.int32)[None, :] < tail_lens[:, None])[:, None, None, :]
        tail_part = attend(queries.reshape(grouped), tail_keys, tail_values, tail_mask)
        new_mask = (offsets[:, None] >= offsets[None, :])[None, :, None, :]
        new_part = attend(queries.reshape(grouped), new_keys.reshape(grouped), new_values.reshape(grouped), new_mask)
        attn_mix = combine([prefix_part, tail_part, new_part]).reshape(per_prompt, head_width).astype(jnp.bfloat16)
        attn_proj = jnp.dot(attn_mix, w_out, preferred_element_type=jnp.float32)
        return (prompt_rows.astype(jnp.float32) + attn_proj).astype(jnp.bfloat16)
    residual = lax.map(one_prompt, jnp.arange(PROMPTS, dtype=jnp.int32)).reshape(TOKENS, D)
    normed_mid = layer_norm(residual.astype(jnp.float32)).astype(jnp.bfloat16)
    layer_f32 = residual.astype(jnp.float32) + swiglu(normed_mid, w_gate, w_up, w_down)
    layer_out = layer_f32.astype(jnp.bfloat16)
    score = lax.optimization_barrier(jnp.sum(layer_norm(layer_f32) * w_score[None, :], axis=-1))
    return (layer_out, score)
```

```python
import functools

import jax
import jax.numpy as jnp
import numpy as np
from jax import lax
from jax.experimental import pallas as pl
from jax.experimental.pallas import tpu as pltpu
from jax.sharding import PartitionSpec as P

MESH = pl.DeviceIdType.MESH
HD = 128
CONT = 16
NEW = 2
NH = 4
T = CONT * NEW
D = 2048
PREFIX = 4096
TAIL = 64
HW = NH * HD
REQ = 32
MLP = 4
HID = 64
CH = 1024
NCH = PREFIX // CH
NEG = -1e30
SCALE = HD ** -0.5
NT = (((1,), (1,)), ((), ()))
F32 = jnp.float32
BF16 = jnp.bfloat16


def layer_norm(values):
    centre = values - jnp.mean(values, axis=-1, keepdims=True)
    spread = jnp.mean(centre * centre, axis=-1, keepdims=True)
    return centre * lax.rsqrt(spread + 1e-05)


def iota(shape, dim):
    return lax.broadcasted_iota(jnp.int32, shape, dim)


def kernel(
    tok_ref, plen_ref, tlen_ref, tsrc_ref, freq_ref, wscore_ref,
    prefix_hbm, tail_hbm, wqkv_hbm, wout_hbm, wg_hbm, wu_hbm, wd_hbm,
    out_ref, score_ref,
    wqkv, kp, vp, tk, tv, wout, w3, s_buf,
    q_send, q_recv, t_send, t_recv, part, z_send, z_recv,
    g_buf, d_send, d_recv, own_half, r_send, r_recv,
    local_sem, qs, qr, ts, tr, ws, wr, zs, zr, gs, gr, fs, dsem, rs, rr,
):
    r = lax.axis_index("req")
    z = lax.axis_index("mlp")
    core = lax.rem(r, 2)
    chip = r // 2
    up = lax.rem(z + 1, MLP)
    down = lax.rem(z + 3, MLP)

    def local(src, dst, i):
        return pltpu.make_async_copy(src, dst, local_sem.at[i])

    def remote(src, dst, ssem, rsem, req, mlp):
        return pltpu.make_async_remote_copy(
            src_ref=src, dst_ref=dst, send_sem=ssem, recv_sem=rsem,
            device_id=(req, mlp), device_id_type=MESH,
        )

    c_qkv = [local(wqkv_hbm.at[i], wqkv.at[i], i) for i in range(3)]
    c_k = [
        local(prefix_hbm.at[0, 0, pl.ds(c * CH, CH)], kp.at[pl.ds(c * CH, CH)], 3 + c)
        for c in range(NCH)
    ]
    c_v = [
        local(prefix_hbm.at[0, 1, pl.ds(c * CH, CH)], vp.at[pl.ds(c * CH, CH)], 7 + c)
        for c in range(NCH)
    ]
    c_tk = local(tail_hbm.at[:, 0], tk, 11)
    c_tv = local(tail_hbm.at[:, 1], tv, 12)
    c_out = local(wout_hbm, wout, 13)
    hbm3 = (wg_hbm, wu_hbm, wd_hbm)
    c_w = [local(hbm3[m], w3.at[m, z], 14 + m) for m in range(3)]
    for copy in c_qkv + c_k + [c_tk, c_tv] + c_v + [c_out] + c_w:
        copy.start()

    barrier = pltpu.get_barrier_semaphore()

    @pl.loop(1, REQ)
    def _(o):
        pl.semaphore_signal(
            barrier, inc=1, device_id=(lax.rem(r + o, REQ), z), device_id_type=MESH
        )

    for other in (up, down):
        pl.semaphore_signal(barrier, inc=1, device_id=(r, other), device_id_type=MESH)
    pl.semaphore_signal(
        barrier, inc=1, device_id=(r, lax.rem(z + 2, MLP)), device_id_type=MESH
    )
    pl.semaphore_wait(barrier, REQ - 1 + MLP - 1)

    w_sends = []
    for m in range(3):
        a = remote(hbm3[m], w3.at[m, z], ws.at[m, 0], wr.at[m, 0], r, up)
        b = remote(hbm3[m], w3.at[m, z], ws.at[m, 1], wr.at[m, 1], r, down)
        a.start()
        b.start()
        w_sends += [a, b]

    def forward(m):
        lo = remote(w3.at[m, down], w3.at[m, down], ws.at[m, 0], wr.at[m, 0], r, up)
        lo.wait_recv()
        a = remote(
            w3.at[m, down, pl.ds(0, HID // 2)], w3.at[m, down, pl.ds(0, HID // 2)],
            ws.at[m, 2], wr.at[m, 2], r, up,
        )
        a.start()
        hi = remote(w3.at[m, up], w3.at[m, up], ws.at[m, 1], wr.at[m, 1], r, down)
        hi.wait_recv()
        b = remote(
            w3.at[m, up, pl.ds(HID // 2, HID // 2)], w3.at[m, up, pl.ds(HID // 2, HID // 2)],
            ws.at[m, 3], wr.at[m, 3], r, down,
        )
        b.start()
        return [a, b]

    tsrc = tsrc_ref[...]
    tlen = tlen_ref[...]
    held = tsrc == r
    held_col = jnp.sum(held.astype(jnp.int32), axis=1, keepdims=True)
    held_len = jnp.sum(jnp.where(held, tlen, 0), axis=1, keepdims=True)
    held_row = jnp.sum(
        jnp.where(iota((REQ, REQ), 0) == iota((REQ, REQ), 1), held_col, 0), axis=0, keepdims=True
    )
    rank_col = jnp.sum(
        jnp.where(iota((REQ, REQ), 1) < iota((REQ, REQ), 0), held_row, 0), axis=1, keepdims=True
    )
    rank_col = jnp.where(held_col > 0, rank_col, -1)
    rank_l = jnp.sum(
        jnp.where(iota((REQ, 256), 0) == iota((REQ, 256), 1) // 8, rank_col, 0),
        axis=0, keepdims=True,
    )
    len_l = jnp.sum(
        jnp.where(rank_col == iota((REQ, CONT * TAIL), 1) // TAIL, held_len, 0),
        axis=0, keepdims=True,
    )
    src_own = tsrc_ref[pl.ds(r, 1), :]
    src_col = jnp.sum(
        jnp.where(iota((CONT, CONT), 0) == iota((CONT, CONT), 1), src_own, 0),
        axis=1, keepdims=True,
    )
    src_l = jnp.sum(
        jnp.where(iota((CONT, 128), 0) == (iota((CONT, 128), 1) // 2) % CONT, src_col, 0),
        axis=0, keepdims=True,
    )
    src_t = jnp.sum(
        jnp.where((iota((128, CONT), 0) // 2) % CONT == iota((128, CONT), 1), src_own, 0),
        axis=1, keepdims=True,
    )
    rank_t = jnp.sum(
        jnp.where(iota((256, REQ), 0) // 8 == iota((256, REQ), 1),
                  jnp.sum(jnp.where(iota((REQ, REQ), 0) == iota((REQ, REQ), 1), rank_col, 0),
                          axis=0, keepdims=True), 0),
        axis=1, keepdims=True,
    )

    def pair(rows, cols, swapped):
        a, b = (iota((rows, cols), 0), iota((rows, cols), 1))
        if swapped:
            a, b = b, a
        return ((a // NH) % NEW == b % NEW) & (a % NH == b // T), a // 8, (b // 2) % CONT

    own_prefix = plen_ref[r]
    own_tail = tlen_ref[pl.ds(r, 1), :]
    tail_col = jnp.sum(
        jnp.where(iota((T, CONT), 0) // NEW == iota((T, CONT), 1), own_tail, 0),
        axis=1, keepdims=True,
    )
    pos = (own_prefix + tail_col + iota((T, 1), 0) % NEW).astype(F32)
    phase = pos * freq_ref[...]
    cos = jnp.cos(phase)
    sin = jnp.where(iota((T, HD), 1) < HD // 2, -1.0, 1.0) * jnp.sin(phase)

    def rope(v):
        return v * cos + pltpu.roll(v, HD // 2, 1) * sin

    x32 = tok_ref[...].astype(F32)
    normed = layer_norm(x32).astype(BF16)
    c_qkv[0].wait()
    proj = jnp.dot(normed, wqkv[0], preferred_element_type=F32)
    qh = [rope(proj[:, h * HD:(h + 1) * HD]).astype(BF16) for h in range(NH)]

    same, slot, _ = pair(REQ * 8, 128, False)
    sel = jnp.where(same & (src_l == slot), 1.0, 0.0).astype(BF16)
    q_all = jnp.concatenate(qh, axis=0)
    q_send[...] = jnp.dot(sel, q_all, preferred_element_type=F32).reshape(REQ, 8, HD)
    q_recv[r] = q_send[r]

    @pl.loop(1, REQ)
    def _(o):
        peer = lax.rem(r + o, REQ)
        remote(q_send.at[peer], q_recv.at[r], qs.at[peer], qr.at[r], peer, z).start()

    c_qkv[1].wait()
    proj = jnp.dot(normed, wqkv[1], preferred_element_type=F32)
    kh = [rope(proj[:, h * HD:(h + 1) * HD]).astype(BF16) for h in range(NH)]
    c_qkv[2].wait()
    vnew = jnp.dot(normed, wqkv[2], preferred_element_type=F32).astype(BF16)

    row, col = iota((T, T), 0), iota((T, T), 1)
    causal = (row // NEW == col // NEW) & (col <= row)
    s_new, top = [], []
    for h in range(NH):
        s = lax.dot_general(qh[h], kh[h], NT, preferred_element_type=F32) * SCALE
        s = jnp.where(causal, s, NEG)
        s_new.append(s)
        top.append(jnp.max(s, axis=-1, keepdims=True))
    for c in range(NCH):
        c_k[c].wait()
        mask = iota((T, CH), 1) + c * CH < own_prefix
        for h in range(NH):
            s = lax.dot_general(
                qh[h], kp[c * CH:(c + 1) * CH, h * HD:(h + 1) * HD], NT,
                preferred_element_type=F32,
            ) * SCALE
            s = jnp.where(mask, s, NEG)
            s_buf[h, :, c * CH:(c + 1) * CH] = s
            top[h] = jnp.maximum(top[h], jnp.max(s, axis=-1, keepdims=True))

    @pl.loop(1, REQ)
    def _(o):
        peer = lax.rem(r + o, REQ)
        remote(q_send.at[peer], q_recv.at[peer], qs.at[peer], qr.at[peer], peer, z).wait()

    same, slot, kk = pair(128, REQ * 8, True)
    gsel = jnp.where(same & (rank_l == iota((128, 256), 0) // 2 % CONT), 1.0, 0.0).astype(BF16)
    q_t = jnp.dot(
        gsel, q_recv[...].reshape(REQ * 8, HD).astype(BF16), preferred_element_type=F32
    ).astype(BF16)
    c_tk.wait()
    c_tv.wait()
    mine = (iota((T, CONT * TAIL), 0) // NEW == iota((T, CONT * TAIL), 1) // TAIL) & (
        iota((T, CONT * TAIL), 1) % TAIL < len_l
    )
    outs, stats = [], []
    lane = iota((T, HD), 1)
    for h in range(NH):
        keys = tk[:, :, h * HD:(h + 1) * HD].reshape(CONT * TAIL, HD)
        s = lax.dot_general(
            q_t[h * T:(h + 1) * T], keys, NT, preferred_element_type=F32
        ) * SCALE
        s = jnp.where(mine, s, NEG)
        m = jnp.max(s, axis=-1, keepdims=True)
        p = jnp.where(mine, jnp.exp(s - m), 0.0)
        l = jnp.sum(p, axis=-1, keepdims=True)
        values = tv[:, :, h * HD:(h + 1) * HD].reshape(CONT * TAIL, HD)
        outs.append(jnp.dot(p.astype(BF16), values, preferred_element_type=F32))
        stats.append(jnp.where(lane == 0, m, jnp.where(lane == 1, l, 0.0)))
    packed = jnp.concatenate(
        [jnp.concatenate(outs, axis=0), jnp.concatenate(stats, axis=0)], axis=1
    )
    same, slot, kk = pair(REQ * 8, 128, False)
    back = jnp.where(same & (rank_t == kk), 1.0, 0.0)
    t_send[...] = jnp.dot(
        back, packed, preferred_element_type=F32, precision=lax.Precision.HIGHEST
    ).reshape(REQ, 8, 2 * HD)
    t_recv[r] = t_send[r]

    @pl.loop(1, REQ)
    def _(o):
        peer = lax.rem(r + o, REQ)
        remote(t_send.at[peer], t_recv.at[r], ts.at[peer], tr.at[r], peer, z).start()

    w_sends += forward(0)

    acc, total = [], []
    for h in range(NH):
        p = jnp.where(causal, jnp.exp(s_new[h] - top[h]), 0.0)
        total.append(jnp.sum(p, axis=-1, keepdims=True))
        acc.append(
            jnp.dot(p.astype(BF16), vnew[:, h * HD:(h + 1) * HD], preferred_element_type=F32)
        )
    for c in range(NCH):
        c_v[c].wait()
        mask = iota((T, CH), 1) + c * CH < own_prefix
        for h in range(NH):
            p = jnp.where(mask, jnp.exp(s_buf[h, :, c * CH:(c + 1) * CH] - top[h]), 0.0)
            total[h] += jnp.sum(p, axis=-1, keepdims=True)
            acc[h] += jnp.dot(
                p.astype(BF16), vp[c * CH:(c + 1) * CH, h * HD:(h + 1) * HD],
                preferred_element_type=F32,
            )

    w_sends += forward(1)

    @pl.loop(1, REQ)
    def _(o):
        peer = lax.rem(r + o, REQ)
        remote(t_send.at[peer], t_recv.at[peer], ts.at[peer], tr.at[peer], peer, z).wait()

    same, slot, _ = pair(128, REQ * 8, True)
    pick = jnp.where(same & (src_t == slot), 1.0, 0.0)
    got = jnp.dot(
        pick, t_recv[...].reshape(REQ * 8, 2 * HD), preferred_element_type=F32,
        precision=lax.Precision.HIGHEST,
    )
    mix = []
    for h in range(NH):
        part_h = got[h * T:(h + 1) * T]
        m_t, l_t = part_h[:, HD:HD + 1], part_h[:, HD + 1:HD + 2]
        overall = jnp.maximum(top[h], m_t)
        a, b = jnp.exp(top[h] - overall), jnp.exp(m_t - overall)
        mix.append(
            ((a * acc[h] + b * part_h[:, :HD]) / (a * total[h] + b * l_t)).astype(BF16)
        )
    mixed = jnp.concatenate(mix, axis=1)
    c_out.wait()
    part[...] = jnp.dot(mixed, wout[...], preferred_element_type=F32).reshape(MLP, 8, D)
    z_send[...] = part[...].astype(BF16)
    z_copies = []
    for i in range(1, MLP):
        peer = lax.rem(z + i, MLP)
        copy = remote(z_send.at[peer], z_recv.at[i - 1], zs.at[i - 1], zr.at[i - 1], r, peer)
        copy.start()
        z_copies.append(copy)
    w_sends += forward(2)
    summed = part[z]
    for i in range(1, MLP):
        z_copies[i - 1].wait()
        summed += z_recv[i - 1].astype(F32)
    own = tok_ref[pl.ds(pl.multiple_of(z * 8, 8), 8), :].astype(F32)
    residual = (own + summed).astype(BF16).astype(F32)
    normed_mid = layer_norm(residual).astype(BF16)

    me = core * 16 + chip
    g_buf[me] = normed_mid
    sib = r + 1 - 2 * core

    @pl.loop(1, 16)
    def _(o):
        other = lax.rem(chip + o, 16)
        remote(
            g_buf.at[me], g_buf.at[me], gs.at[o], gr.at[me], other * 2 + core, z
        ).start()

    first = remote(g_buf.at[me], g_buf.at[me], fs.at[0], gr.at[me], sib, z)
    first.start()

    @pl.loop(1, 16)
    def _(o):
        theirs = core * 16 + lax.rem(chip + o, 16)
        remote(g_buf.at[theirs], g_buf.at[theirs], gs.at[o], gr.at[theirs], sib, z).wait_recv()
        remote(g_buf.at[theirs], g_buf.at[theirs], fs.at[o], gr.at[theirs], sib, z).start()

    @pl.loop(0, 16)
    def _(o):
        theirs = (1 - core) * 16 + lax.rem(chip + o, 16)
        remote(g_buf.at[theirs], g_buf.at[theirs], fs.at[o], gr.at[theirs], sib, z).wait_recv()

    @pl.loop(0, 16)
    def _(o):
        remote(g_buf.at[me], g_buf.at[me], fs.at[o], gr.at[me], sib, z).wait_send()

    @pl.loop(1, 16)
    def _(o):
        remote(g_buf.at[me], g_buf.at[me], gs.at[o], gr.at[me], sib, z).wait_send()

    opp = lax.rem(z + 2, MLP)
    for m in range(3):
        c_w[m].wait()
        a = w3.at[m, opp, pl.ds(0, HID // 2)]
        b = w3.at[m, opp, pl.ds(HID // 2, HID // 2)]
        remote(a, a, ws.at[m, 2], wr.at[m, 2], r, up).wait_recv()
        remote(b, b, ws.at[m, 3], wr.at[m, 3], r, down).wait_recv()
    for copy in w_sends:
        copy.wait_send()

    def mlp(side):
        rows = g_buf[pl.ds(side * 16, 16)].reshape(128, D)
        wg = w3[0].reshape(MLP * HID, D)
        wu = w3[1].reshape(MLP * HID, D)
        wd = w3[2].reshape(MLP * HID, D)
        gate = lax.dot_general(rows, wg, NT, preferred_element_type=F32)
        upper = lax.dot_general(rows, wu, NT, preferred_element_type=F32)
        hidden = (gate / (1.0 + jnp.exp(-gate)) * upper).astype(BF16)
        return jnp.dot(hidden, wd, preferred_element_type=F32).reshape(16, 8, D)

    d_send[...] = mlp(1 - core).astype(BF16)
    d_copy = remote(d_send, d_recv, dsem.at[0], dsem.at[1], sib, z)
    d_copy.start()
    own_half[...] = mlp(core)
    d_copy.wait()
    own_half[...] += d_recv[...].astype(F32)
    r_send[...] = own_half[...].astype(BF16)

    @pl.loop(1, 16)
    def _(o):
        other = lax.rem(chip + o, 16)
        remote(
            r_send.at[other], r_recv.at[chip], rs.at[o], rr.at[chip], other * 2 + core, z
        ).start()

    r_recv[chip] = jnp.zeros((8, D), BF16)

    @pl.loop(1, 16)
    def _(o):
        other = lax.rem(chip + o, 16)
        remote(
            r_send.at[other], r_recv.at[other], rs.at[o], rr.at[other], other * 2 + core, z
        ).wait()

    layer = residual + own_half[chip]
    for i in range(16):
        layer += r_recv[i].astype(F32)
    out_ref[...] = layer.astype(BF16)
    score_ref[...] = jnp.sum(layer_norm(layer) * wscore_ref[...], axis=-1, keepdims=True)


def on_device(
    tokens, prefix_len, tail_len, tail_src, prefix_kv, tail_kv,
    w_qkv, w_out, w_gate, w_up, w_down, w_score,
):
    exponent = np.arange(HD // 2, dtype=np.float32) * np.float32(2.0 / HD)
    freq = np.power(np.float32(10000.0), -exponent).astype(np.float32)
    freq = jnp.asarray(np.concatenate([freq, freq])[None, :])
    vmem = pl.BlockSpec(memory_space=pltpu.VMEM)
    smem = pl.BlockSpec(memory_space=pltpu.SMEM)
    hbm = pl.BlockSpec(memory_space=pl.ANY)
    dma = pltpu.SemaphoreType.DMA
    out, score = pl.pallas_call(
        kernel,
        out_shape=(
            jax.ShapeDtypeStruct((8, D), BF16),
            jax.ShapeDtypeStruct((8, 1), F32),
        ),
        in_specs=[vmem, smem, vmem, vmem, vmem, vmem] + [hbm] * 7,
        out_specs=(vmem, vmem),
        scratch_shapes=[
            pltpu.VMEM((3, D, HW), BF16),
            pltpu.VMEM((PREFIX, HW), BF16),
            pltpu.VMEM((PREFIX, HW), BF16),
            pltpu.VMEM((CONT, TAIL, HW), BF16),
            pltpu.VMEM((CONT, TAIL, HW), BF16),
            pltpu.VMEM((HW, D), BF16),
            pltpu.VMEM((3, MLP, HID, D), BF16),
            pltpu.VMEM((NH, T, PREFIX), F32),
            pltpu.VMEM((REQ, 8, HD), F32),
            pltpu.VMEM((REQ, 8, HD), F32),
            pltpu.VMEM((REQ, 8, 2 * HD), F32),
            pltpu.VMEM((REQ, 8, 2 * HD), F32),
            pltpu.VMEM((MLP, 8, D), F32),
            pltpu.VMEM((MLP, 8, D), BF16),
            pltpu.VMEM((MLP - 1, 8, D), BF16),
            pltpu.VMEM((REQ, 8, D), BF16),
            pltpu.VMEM((16, 8, D), BF16),
            pltpu.VMEM((16, 8, D), BF16),
            pltpu.VMEM((16, 8, D), F32),
            pltpu.VMEM((16, 8, D), BF16),
            pltpu.VMEM((16, 8, D), BF16),
            dma((17,)),
            dma((REQ,)), dma((REQ,)), dma((REQ,)), dma((REQ,)),
            dma((3, 4)), dma((3, 4)),
            dma((MLP - 1,)), dma((MLP - 1,)),
            dma((16,)), dma((REQ,)), dma((16,)),
            dma((2,)),
            dma((16,)), dma((16,)),
        ],
        compiler_params=pltpu.CompilerParams(
            collective_id=0, has_side_effects=True, vmem_limit_bytes=56 * 1024 * 1024
        ),
        name="layer",
    )(
        tokens, prefix_len, tail_len, tail_src.reshape(REQ, CONT), freq,
        w_score.reshape(1, D),
        prefix_kv, tail_kv, jnp.transpose(w_qkv, (1, 0, 2)), w_out, w_gate, w_up, w_down,
    )
    return out, score.reshape(8)


def solution(mesh):
    in_specs = (
        P("req", None),
        P(),
        P(),
        P(),
        P("req", None, None, "mlp"),
        P("req", None, None, "mlp"),
        P(None, None, "mlp"),
        P("mlp", None),
        P(("req", "mlp"), None),
        P(("req", "mlp"), None),
        P(("req", "mlp"), None),
        P(),
    )
    out_specs = (P(("req", "mlp"), None), P(("req", "mlp")))
    return jax.shard_map(
        on_device, mesh=mesh, in_specs=in_specs, out_specs=out_specs, check_vma=False
    )
```
